32 devices in a mesh: groups: 2 (over y), dp: 4 (over x, core), expert: 4 (over z).
Axes of the slice: x: 2, y: 2, z: 4, core: 2. Of those that a mesh axis runs over, the one named last changes fastest.
Arguments:
- tokens: bfloat16 [256, 2048], P(('groups', 'dp', 'expert')), parts along dimension 0, may hold values from -3.5 to 3.5
- routes: int32 [256, 8], P('groups'), parts along dimension 0, may hold values from 0 to 15, all different within a row; in each aligned block of 8 rows (0 to 7, 8 to 15, ...) at most 8 rows name the same one
- gates: float32 [256, 8], P(('groups', 'dp', 'expert')), parts along dimension 0, may hold values from 0.1 to 1
- valid: int32 [256], P('groups'), parts along dimension 0, may hold values 0 or 1
- norm_gain: float32 [2048], replicated, may hold values from 0.5 to 1.5
- final_gain: float32 [2048], replicated, may hold values from 0.5 to 1.5
- w_gate: bfloat16 [16, 2048, 1024], P('expert', None, 'dp'), may hold values from -0.125 to 0.125
- w_up: bfloat16 [16, 2048, 1024], P('expert', None, 'dp'), may hold values from -0.125 to 0.125
- w_down: bfloat16 [16, 1024, 2048], P('expert', 'dp'), may hold values from -0.1875 to 0.1875
- head_weight: bfloat16 [2048, 10240], P(None, ('dp', 'expert')), as said below
- student_logits: bfloat16 [256, 10240], P('groups', ('dp', 'expert')), parts along dimension 0, may hold values from -24 to 220
Outputs:
- reverse_kl: float32 [256], P('groups'), parts along dimension 0
- logit_grad: bfloat16 [256, 10240], P('groups', ('dp', 'expert')), parts along dimension 0
The draws below stay inside these ranges and needn't reach their ends.
There are 2 independent parts, one for each index of `groups`. The reference program is written for one: setup_inputs(seed, part) draws one part's arguments, and reference() takes and returns one part's arrays. A program takes and returns all parts, laid end to end along the dimension named above; an argument that names none is the same for every part. Nothing has to cross between parts.
Inputs may be any that keep to these rules, and one draw needn't show every extreme that they name: Each token names 8 different experts. In the 8 tokens of one device (aligned blocks of rows), no expert is named by more than 8 routes, a bound that some block reaches. `head_weight`: entries are of order one over the square root of 2048.
All inputs are finite; a program needn't handle non-finite values.
Results may differ from the reference program's by a relative error of at most 0.015.
Values may be sent and summed in bfloat16 or wider, within the bound.
No kernel may reach another device: no remote copies, remote signals or barrier semaphores. Data moves between devices by JAX's collectives and lax.ppermute only.
A program may use at most 64 MiB of HBM per device.

```python
import math
import jax
import jax.numpy as jnp
import numpy as np
from jax import lax

D = 2048
FF = 1024
TOP = 8
TOK_DEV = 8
EXPERTS = 16
TOKENS = 128
VOCAB = 10240
CAP = 8
N_DP = 4
N_EXPERT = 4


def draw_tokens(key, part):
    noise_key = jax.random.fold_in(key, 0)
    noise_part = 0.5 * jax.random.normal(noise_key, (TOKENS, D), jnp.float32)
    return jnp.clip(noise_part, -3.0, 3.0).astype(jnp.bfloat16)


def draw_head_weight(key, part):
    noise_key = jax.random.fold_in(key, 0)
    rising = 1.0 + 2.0 * jnp.arange(VOCAB, dtype=jnp.float32) / VOCAB
    scale_root = jnp.sqrt(jnp.float32(D))
    noise_part = jnp.clip(jax.random.normal(noise_key, (D, VOCAB), jnp.float32), -4.0, 4.0)
    return (noise_part * rising[None, :] / scale_root).astype(jnp.bfloat16)


def draw_student_logits(key, part):
    subkeys = jax.random.split(key, 2)
    rising = 1.0 + 2.0 * jnp.arange(VOCAB, dtype=jnp.float32) / VOCAB
    row_scales = jnp.exp(jax.random.uniform(subkeys[0], (TOKENS, 1), jnp.float32, 0.0, jnp.log(2.0)))
    base_logits = 1.2 * jax.random.normal(subkeys[1], (TOKENS, VOCAB), jnp.float32) * rising[None, :] * row_scales
    return jnp.clip(base_logits, -14.0, 14.0).astype(jnp.bfloat16)


def plant(result, rng, least, largest):
    longest = result.shape.index(max(result.shape))
    spots = []
    for shift in (0, 1):
        where = [jax.random.randint(jax.random.fold_in(rng, axis), (), 0, length) for axis, length in enumerate(result.shape)]
        where[longest] = (where[longest] + shift) % result.shape[longest]
        spots.append(tuple(where))
    return result.at[spots[0]].set(least).at[spots[1]].set(largest)


def shard_levels(own_key, shape, pieces, smallest, largest):
    level, own = 1.0, jax.random.fold_in(own_key, 6)
    for axis_at, parts in pieces:
        heights = jnp.exp(jax.random.uniform(jax.random.fold_in(own, axis_at), (parts,), jnp.float32, smallest / len(pieces), largest / len(pieces)))
        level = level * jnp.repeat(heights, shape[axis_at] // parts).reshape([-1 if axis == axis_at else 1 for axis in range(len(shape))])
    return level


def assign_block(stream_key, own, number, rows, amount, top, limit, lean):
    order = jax.random.permutation(stream_key, amount)
    heavy_load, ordinary = portions_of(amount, rows * top, limit, lean, True), portions_of(amount, rows * top, limit, lean, False)
    places = jnp.arange(amount)

    def named(lengths, rotation):
        used = int((lengths > 0).sum())
        fixed = max(1, used // 4)
        shifted = fixed + (places - fixed + rotation * (used - fixed)) % max(1, amount - fixed)
        return jnp.zeros((amount,), jnp.int32).at[order[jnp.where(places < fixed, places, shifted)]].set(jnp.asarray(lengths, jnp.int32))

    lengths = jnp.where(number % 4 == 0, named(heavy_load, number // 4), named(ordinary, number - number // 4 - 1))
    mixed = jax.random.permutation(jax.random.fold_in(own, 3), amount)
    source_of, taker = mixed[0:amount // 2 * 2:2], mixed[1:amount // 2 * 2:2]
    room = jnp.minimum(lengths[source_of] - 1, limit - lengths[taker]) // 2
    room = jnp.where((source_of == order[0]) | (taker == order[0]) | (lengths[taker] == 0), 0, jnp.maximum(room, 0))
    shifted = jax.random.randint(jax.random.fold_in(own, 4), (amount // 2,), 0, 1 << 20) % (room + 1)
    lengths = lengths.at[source_of].add(-shifted).at[taker].add(shifted)
    members = jnp.searchsorted(jnp.cumsum(lengths), jnp.arange(rows * top), side="right").astype(jnp.int32)
    table = members.reshape(top, rows).T
    table = table[jax.random.permutation(jax.random.fold_in(own, 1), rows)]
    rotation = jax.random.randint(jax.random.fold_in(own, 2), (rows, 1), 0, top)
    return jnp.take_along_axis(table, (jnp.arange(top)[None, :] + rotation) % top, axis=1)


def portions_of(count, total, reach, lean, full):
    loads = [(1 << 20) // math.isqrt(grade ** lean) + 1 for grade in range(1, count + 1)]
    largest = reach if full else min(reach, max(-(-total // count), total * loads[0] // sum(loads)))
    least = 1 if total - largest >= count - 1 else 0
    holding, spare = [largest] + [least] * (count - 1), total - largest - least * (count - 1)
    while spare > 0:
        free = [i for i in range(1, count) if holding[i] < largest] or [i for i in range(1, count) if holding[i] < reach]
        pool, budget = sum([loads[i] for i in free]), spare
        for i in free:
            extra = min(reach - holding[i], max(1, budget * loads[i] // pool), spare)
            holding[i] = holding[i] + extra
            spare = spare - extra
    return np.array(holding)


def normal_values(stream_key, shape, scale, most, pieces=(), held_as=jnp.bfloat16):
    entries = jax.random.normal(stream_key, shape, jnp.float32) * scale
    if len(pieces) > 0:
        entries = shard_levels(stream_key, shape, pieces, -0.22, 0.18) * entries
    return jnp.clip(entries, min=-most, max=most).astype(held_as)


def setup_inputs(seed: int = 0, part: int = 0) -> dict:
    splits = jax.random.split(jax.random.key(seed), 12)
    part_splits = jax.random.split(jax.random.fold_in(splits[11], part), 12)
    tokens = draw_tokens(jax.random.fold_in(jax.random.fold_in(splits[11], part), 71), part)
    routes_keys = jax.random.split(jax.random.fold_in(part_splits[1], 1), TOKENS // TOK_DEV)
    routes_turns = jax.random.permutation(jax.random.fold_in(part_splits[1], 3), TOKENS // TOK_DEV)
    routes = jax.vmap(lambda own, number: assign_block(jax.random.fold_in(part_splits[1], 2), own, number, TOK_DEV, EXPERTS, TOP, CAP, 2))(routes_keys, routes_turns).reshape((TOKENS, TOP))
    gates = jnp.clip(jnp.exp(math.log(1.0) - 2.3025851 * jax.random.uniform(part_splits[2], (TOKENS, TOP), jnp.float32) ** shard_levels(part_splits[2], (TOKENS, TOP), ((0, 16),), -0.2, 0.2)), 0.1, 1.0)
    valid = plant((jax.random.randint(part_splits[3], (TOKENS,), 0, 4) < 3).astype(jnp.int32), jax.random.fold_in(part_splits[3], 1), 0, 1)
    norm_gain = jnp.clip(1.0 + 0.1 * jax.random.normal(splits[4], (D,), jnp.float32), 0.5, 1.5)
    final_gain = jnp.clip(1.0 + 0.1 * jax.random.normal(splits[5], (D,), jnp.float32), 0.5, 1.5)
    w_gate = normal_values(splits[6], (EXPERTS, D, FF), D ** -0.5, 0.125, ((0, 4), (2, 4)))
    w_up = normal_values(splits[7], (EXPERTS, D, FF), D ** -0.5, 0.125, ((0, 4), (2, 4)))
    w_down = normal_values(splits[8], (EXPERTS, FF, D), FF ** -0.5, 0.1875, ((0, 4), (1, 4)))
    head_weight = draw_head_weight(jax.random.fold_in(splits[11], 71), part)
    student_logits = draw_student_logits(jax.random.fold_in(jax.random.fold_in(splits[11], part), 71), part)
    return {"tokens": tokens, "routes": routes, "gates": gates, "valid": valid, "norm_gain": norm_gain, "final_gain": final_gain, "w_gate": w_gate, "w_up": w_up, "w_down": w_down, "head_weight": head_weight, "student_logits": student_logits}


epsilon = 1e-06

def rms_scale(values, gain_vector):
    mean_square = lax.optimization_barrier(jnp.mean(values * values, axis=-1, keepdims=True))
    return values * lax.rsqrt(mean_square + epsilon) * gain_vector

def reference(tokens, routes, gates, valid, norm_gain, final_gain, w_gate, w_up, w_down, head_weight, student_logits):
    hidden_in = tokens.astype(jnp.float32)
    normed = rms_scale(hidden_in, norm_gain).astype(jnp.bfloat16)
    weights = gates / lax.optimization_barrier(jnp.sum(gates, axis=1, keepdims=True))
    flat_routes = routes.reshape(-1)
    flat_weights = weights.reshape(-1)
    route_total = TOKENS * TOP
    most_rows = CAP * N_DP * N_EXPERT

    def one_expert(combined, expert):
        picked = jnp.nonzero(flat_routes == expert, size=most_rows, fill_value=route_total)[0].astype(jnp.int32)
        live_rows = picked < route_total
        token_ids = jnp.minimum(picked // TOP, TOKENS - 1).astype(jnp.int32)
        row_block = normed[token_ids]
        gate_part = jnp.dot(row_block, w_gate[expert], preferred_element_type=jnp.float32)
        up_part = jnp.dot(row_block, w_up[expert], preferred_element_type=jnp.float32)
        activation = (jax.nn.silu(gate_part) * up_part).astype(jnp.bfloat16)
        expert_out = jnp.dot(activation, w_down[expert], preferred_element_type=jnp.float32).astype(jnp.bfloat16)
        expert_out = lax.optimization_barrier(expert_out).astype(jnp.float32)
        safe_index = jnp.minimum(picked, route_total - 1).astype(jnp.int32)
        route_scale = jnp.where(live_rows, flat_weights[safe_index], jnp.zeros_like(flat_weights[safe_index]))
        combined = combined.at[token_ids].add(route_scale[:, None] * expert_out)
        return (combined, None)
    combined, _ = lax.scan(one_expert, jnp.zeros((TOKENS, D), jnp.float32), jnp.arange(EXPERTS, dtype=jnp.int32))
    mixed = hidden_in + combined
    final_normed = rms_scale(mixed, final_gain).astype(jnp.bfloat16)
    teacher = jnp.dot(final_normed, head_weight, preferred_element_type=jnp.float32)
    student = student_logits.astype(jnp.float32)
    teacher_top = lax.optimization_barrier(jnp.max(teacher, axis=1, keepdims=True))
    student_top = lax.optimization_barrier(jnp.max(student, axis=1, keepdims=True))
    log_teacher = teacher_top + jnp.log(lax.optimization_barrier(jnp.sum(jnp.exp(teacher - teacher_top), axis=1, keepdims=True)))
    log_student = student_top + jnp.log(lax.optimization_barrier(jnp.sum(jnp.exp(student - student_top), axis=1, keepdims=True)))
    student_prob = jnp.exp(student - log_student)
    divergence = lax.optimization_barrier(jnp.sum(student_prob * (student - teacher), axis=1, keepdims=True)) - log_student + log_teacher
    valid_rows = valid.astype(jnp.float32)[:, None]
    logit_grad = (valid_rows * student_prob * (student - log_student - (teacher - log_teacher) - divergence)).astype(jnp.bfloat16)
    return ((valid_rows * divergence)[:, 0], logit_grad)
```

```python
import jax
import jax.numpy as jnp
from jax import lax
from jax.sharding import PartitionSpec as P

epsilon = 1e-06


def rms_scale(values, gain_vector):
    mean_square = jnp.mean(values * values, axis=-1, keepdims=True)
    return values * lax.rsqrt(mean_square + epsilon) * gain_vector


def swap(value, axis, mask):
    size = lax.axis_size(axis)
    return lax.ppermute(value, axis, [(i, i ^ mask) for i in range(size)])


def gather_relative(block, axis):
    size = lax.axis_size(axis)
    if size <= 4:
        return [block] + [swap(block, axis, mask) for mask in range(1, size)]
    blocks = [block]
    mask = 1
    while mask < size:
        stacked = jnp.stack(blocks)
        other = swap(stacked, axis, mask)
        blocks = blocks + [other[i] for i in range(mask)]
        mask *= 2
    return blocks


def scatter_relative(blocks, axis):
    size = lax.axis_size(axis)
    if size <= 4:
        parts = [swap(blocks[mask], axis, mask) for mask in range(1, size)]
        total = blocks[0].astype(jnp.float32)
        for part in parts:
            total = total + part.astype(jnp.float32)
        return total
    mask = size // 2
    while mask >= 1:
        other = swap(blocks[mask : 2 * mask].astype(jnp.bfloat16), axis, mask)
        blocks = blocks[:mask].astype(jnp.float32) + other.astype(jnp.float32)
        mask //= 2
    return blocks[0]


def in_order(blocks, index):
    mask = 1
    while mask < len(blocks):
        bit = (index & mask) != 0
        blocks = [jnp.where(bit, blocks[r ^ mask], blocks[r]) for r in range(len(blocks))]
        mask *= 2
    return jnp.stack(blocks)


def three_way(values):
    high = lax.reduce_precision(values, 8, 7)
    rest = values - high
    middle = lax.reduce_precision(rest, 8, 7)
    low = rest - middle
    return [part.astype(jnp.bfloat16) for part in (high, middle, low)]


def body(
    tokens,
    routes,
    gates,
    valid,
    norm_gain,
    final_gain,
    w_gate,
    w_up,
    w_down,
    head_weight,
    student_logits,
):
    rows, width = tokens.shape
    top = routes.shape[1]
    n_dp, n_ex = lax.axis_size("dp"), lax.axis_size("expert")
    dp_at, ex_at = lax.axis_index("dp"), lax.axis_index("expert")
    local, hidden = w_gate.shape[0], w_gate.shape[2]
    count = rows * n_dp * n_ex
    own_routes = lax.dynamic_slice_in_dim(routes, (dp_at * n_ex + ex_at) * rows, rows, 0)
    extra = three_way(gates) + [own_routes.astype(jnp.bfloat16)]
    extra.append(jnp.zeros((rows, -4 * top % 128), jnp.bfloat16))
    packed = jnp.concatenate([tokens] + extra, axis=1)

    along_ex = jnp.stack(gather_relative(packed, "expert"))
    everyone = jnp.stack(gather_dp(along_ex)).reshape(count, packed.shape[1])
    x = everyone[:, :width].astype(jnp.float32)
    side = everyone[:, width : width + 4 * top].astype(jnp.float32).reshape(count, 4, top)
    gate_all = side[:, 0] + side[:, 1] + side[:, 2]
    weight_all = gate_all / jnp.sum(gate_all, axis=1, keepdims=True)
    experts = ex_at * local + jnp.arange(local, dtype=jnp.int32)
    named = side[:, 3][:, :, None] == experts.astype(jnp.float32)[None, None, :]
    scale = jnp.sum(jnp.where(named, weight_all[:, :, None], 0.0), axis=1)

    normed = rms_scale(x, norm_gain).astype(jnp.bfloat16)
    gate_part = jnp.einsum("td,ldf->tlf", normed, w_gate, preferred_element_type=jnp.float32)
    up_part = jnp.einsum("td,ldf->tlf", normed, w_up, preferred_element_type=jnp.float32)
    activation = jax.nn.silu(gate_part) * up_part
    activation = jnp.where(scale[:, :, None] != 0, activation * scale[:, :, None], 0.0)
    partial = jnp.dot(
        activation.astype(jnp.bfloat16).reshape(count, local * hidden),
        w_down.reshape(local * hidden, width),
        preferred_element_type=jnp.float32,
    )
    partial = partial.reshape(n_dp, n_ex, rows, width).astype(jnp.bfloat16)
    mine = partial
    mask = 1
    sums = mine
    mine = scatter_dp(sums, n_dp)
    combined = scatter_relative(mine.astype(jnp.bfloat16), "expert")
    mixed = tokens.astype(jnp.float32) + combined
    final_normed = rms_scale(mixed, final_gain).astype(jnp.bfloat16)

    along_ex = in_order(gather_relative(final_normed, "expert"), ex_at)
    everyone = in_order(gather_dp(along_ex), dp_at).reshape(count, width)
    teacher = jnp.dot(everyone, head_weight, preferred_element_type=jnp.float32)

    student = student_logits.astype(jnp.float32)
    student_top = jnp.max(student, axis=1)
    student_exp = jnp.exp(student - student_top[:, None])
    student_sum = jnp.sum(student_exp, axis=1)
    teacher_top = jnp.max(teacher, axis=1)
    teacher_sum = jnp.sum(jnp.exp(teacher - teacher_top[:, None]), axis=1)
    cross = jnp.sum(student_exp * (student - teacher), axis=1)
    own = jnp.stack([student_top, student_sum, teacher_top, teacher_sum, cross])
    ranks = n_dp * n_ex
    shared = lax.all_to_all(
        jnp.broadcast_to(own[None], (ranks,) + own.shape), ("dp", "expert"), 0, 0, tiled=True
    )
    s_top, t_top = jnp.max(shared[:, 0], axis=0), jnp.max(shared[:, 2], axis=0)
    s_part = jnp.exp(shared[:, 0] - s_top)
    s_total = jnp.sum(s_part * shared[:, 1], axis=0)
    t_total = jnp.sum(jnp.exp(shared[:, 2] - t_top) * shared[:, 3], axis=0)
    cross_total = jnp.sum(s_part * shared[:, 4], axis=0)
    log_student = s_top + jnp.log(s_total)
    log_teacher = t_top + jnp.log(t_total)
    divergence = cross_total / s_total - log_student + log_teacher
    live = valid.astype(jnp.float32)
    prob = jnp.exp(student - log_student[:, None])
    shift = (log_teacher - log_student - divergence)[:, None]
    grad = live[:, None] * prob * (student - teacher + shift)
    return live * divergence, grad.astype(jnp.bfloat16)


def gather_dp(block):
    size = lax.axis_size("dp")
    blocks = [block]
    if size == 4:
        far = swap(block, "dp", 2)
        near = swap(block, "dp", 1)
        return [block, near, far, swap(far, "dp", 1)]
    mask = size // 2
    stacked = block[None]
    while mask >= 1:
        other = swap(stacked, "dp", mask)
        stacked = jnp.stack([stacked, other], axis=1).reshape((-1,) + block.shape)
        mask //= 2
    return [stacked[i] for i in range(size)]


def scatter_dp(blocks, size):
    mask = 1
    while mask < size:
        pairs = blocks.reshape((blocks.shape[0] // 2, 2) + blocks.shape[1:])
        other = swap(pairs[:, 1].astype(jnp.bfloat16), "dp", mask)
        blocks = pairs[:, 0].astype(jnp.float32) + other.astype(jnp.float32)
        mask *= 2
    return blocks[0]


def solution(mesh):
    placed = (
        P(("groups", "dp", "expert"), None),
        P("groups", None),
        P(("groups", "dp", "expert"), None),
        P("groups"),
        P(),
        P(),
        P("expert", None, "dp"),
        P("expert", None, "dp"),
        P("expert", "dp", None),
        P(None, ("dp", "expert")),
        P("groups", ("dp", "expert")),
    )
    return jax.shard_map(
        body,
        mesh=mesh,
        in_specs=placed,
        out_specs=(P("groups"), P("groups", ("dp", "expert"))),
        check_vma=False,
    )
```

```python
import functools

import jax
import jax.numpy as jnp
from jax import lax
from jax.experimental import pallas as pl
from jax.experimental.pallas import tpu as pltpu
from jax.sharding import PartitionSpec as P

epsilon = 1e-06


def rms_scale(values, gain_vector):
    mean_square = jnp.mean(values * values, axis=-1, keepdims=True)
    return values * lax.rsqrt(mean_square + epsilon) * gain_vector


def swap(value, axis, mask):
    size = lax.axis_size(axis)
    return lax.ppermute(value, axis, [(i, i ^ mask) for i in range(size)])


def gather_relative(block, axis):
    size = lax.axis_size(axis)
    if size <= 4:
        return [block] + [swap(block, axis, mask) for mask in range(1, size)]
    blocks = [block]
    mask = 1
    while mask < size:
        stacked = jnp.stack(blocks)
        other = swap(stacked, axis, mask)
        blocks = blocks + [other[i] for i in range(mask)]
        mask *= 2
    return blocks


def scatter_relative(blocks, axis):
    size = lax.axis_size(axis)
    if size <= 4:
        parts = [swap(blocks[mask], axis, mask) for mask in range(1, size)]
        total = blocks[0].astype(jnp.float32)
        for part in parts:
            total = total + part.astype(jnp.float32)
        return total
    mask = size // 2
    while mask >= 1:
        other = swap(blocks[mask : 2 * mask].astype(jnp.bfloat16), axis, mask)
        blocks = blocks[:mask].astype(jnp.float32) + other.astype(jnp.float32)
        mask //= 2
    return blocks[0]


def in_order(blocks, index):
    mask = 1
    while mask < len(blocks):
        bit = (index & mask) != 0
        blocks = [jnp.where(bit, blocks[r ^ mask], blocks[r]) for r in range(len(blocks))]
        mask *= 2
    return jnp.stack(blocks)


def pack_kernel(expert_count, tokens_hbm, routes_hbm, gates_hbm, packed_ref, routes_ref, gates_ref, sems):
    width = tokens_hbm.shape[1]
    copies = [
        pltpu.make_async_copy(routes_hbm, routes_ref, sems.at[0]),
        pltpu.make_async_copy(gates_hbm, gates_ref, sems.at[1]),
        pltpu.make_async_copy(tokens_hbm, packed_ref.at[:, pl.ds(0, width)], sems.at[2]),
    ]
    for copy in copies:
        copy.start()
    for copy in copies:
        copy.wait()
    rows = tokens_hbm.shape[0]
    top, count = routes_ref.shape
    extra = packed_ref.shape[1] - width
    position = lax.axis_index("dp") * lax.axis_size("expert") + lax.axis_index("expert")
    column = lax.broadcasted_iota(jnp.int32, (rows, count), 1)
    row = lax.broadcasted_iota(jnp.int32, (rows, count), 0)
    pick = (column == position * rows + row).astype(jnp.float32)
    own_routes = lax.dot_general(
        pick, routes_ref[...].astype(jnp.float32), (((1,), (1,)), ((), ())),
        preferred_element_type=jnp.float32,
    )
    gates = gates_ref[...]
    weights = gates / jnp.sum(gates, axis=1, keepdims=True)
    lane = lax.broadcasted_iota(jnp.int32, (rows, extra), 1)
    expert = lax.rem(lane, expert_count).astype(jnp.float32)
    dense = jnp.zeros((rows, extra), jnp.float32)
    for k in range(top):
        dense = dense + jnp.where(own_routes[:, k : k + 1] == expert, weights[:, k : k + 1], 0.0)
    high = dense.astype(jnp.bfloat16).astype(jnp.float32)
    middle = (dense - high).astype(jnp.bfloat16).astype(jnp.float32)
    low = dense - high - middle
    side = jnp.where(lane < expert_count, high, jnp.where(lane < 2 * expert_count, middle, low))
    packed_ref[:, width:] = jnp.where(lane < 3 * expert_count, side, 0.0).astype(jnp.bfloat16)


def pack(tokens, routes, gates, expert_count):
    rows, width = tokens.shape
    extra = -(-3 * expert_count // 128) * 128
    return pl.pallas_call(
        functools.partial(pack_kernel, expert_count),
        out_shape=jax.ShapeDtypeStruct((rows, width + extra), jnp.bfloat16),
        in_specs=[pl.BlockSpec(memory_space=pltpu.HBM)] * 3,
        out_specs=pl.BlockSpec(memory_space=pltpu.VMEM),
        scratch_shapes=[
            pltpu.VMEM(routes.shape[::-1], jnp.int32),
            pltpu.VMEM(gates.shape, jnp.float32),
            pltpu.SemaphoreType.DMA((3,)),
        ],
        compiler_params=pltpu.CompilerParams(vmem_limit_bytes=4 << 20),
        name="pack",
    )(*[pltpu.with_memory_space_constraint(array, pltpu.HBM) for array in (tokens, routes.T, gates)])


def fetch_kernel(amount, *refs):
    sources, targets, sems = refs[:amount], refs[amount : 2 * amount], refs[2 * amount]
    copies = [pltpu.make_async_copy(sources[i], targets[i], sems.at[i]) for i in range(amount)]
    for copy in copies:
        copy.start()
    for copy in copies:
        copy.wait()


def fetch(*arrays):
    size = sum(2 * array.size for array in arrays)
    return pl.pallas_call(
        functools.partial(fetch_kernel, len(arrays)),
        out_shape=tuple(pltpu.VMEM(array.shape, array.dtype) for array in arrays),
        in_specs=[pl.BlockSpec(memory_space=pltpu.HBM)] * len(arrays),
        out_specs=tuple(pl.BlockSpec(memory_space=pltpu.VMEM) for array in arrays),
        scratch_shapes=[pltpu.SemaphoreType.DMA((len(arrays),))],
        compiler_params=pltpu.CompilerParams(vmem_limit_bytes=size + (4 << 20)),
        cost_estimate=pl.CostEstimate(flops=0, bytes_accessed=size, transcendentals=0),
        name="fetch",
    )(*[pltpu.with_memory_space_constraint(array, pltpu.HBM) for array in arrays])


def experts_kernel(expert_count, pieces, *refs):
    piece_refs, refs = refs[:pieces], refs[pieces:]
    gain_ref, gate_ref, up_ref, down_ref, keep_ref, send_ref, normed, side, active = refs
    local, width, hidden = gate_ref.shape
    half = keep_ref.shape[0]
    block = piece_refs[0].shape[0] * piece_refs[0].shape[1]
    gain = gain_ref[...]
    for i, ref in enumerate(piece_refs):
        value = ref[...].astype(jnp.float32).reshape(block, ref.shape[2])
        x = value[:, :width]
        mean_square = jnp.sum(x * x, axis=1, keepdims=True) * (1.0 / width)
        scaled = x * lax.rsqrt(mean_square + epsilon) * gain
        normed[i * block : (i + 1) * block, :] = scaled.astype(jnp.bfloat16)
        side[i * block : (i + 1) * block, :] = value[:, width:].astype(jnp.bfloat16)
    first = lax.axis_index("expert") * local
    slot = lax.rem(lax.broadcasted_iota(jnp.int32, (side.shape[1], hidden), 0), expert_count)
    for i in range(local):
        select = (slot == first + i).astype(jnp.float32).astype(jnp.bfloat16)
        scale = jnp.dot(side[...], select, preferred_element_type=jnp.float32)
        gate_part = jnp.dot(normed[...], gate_ref[i], preferred_element_type=jnp.float32)
        up_part = jnp.dot(normed[...], up_ref[i], preferred_element_type=jnp.float32)
        value = gate_part / (1.0 + jnp.exp(-gate_part)) * up_part * scale
        active[:, i * hidden : (i + 1) * hidden] = value.astype(jnp.bfloat16)
    step = width // 4
    for i in range(4):
        columns = slice(i * step, (i + 1) * step)
        part = jnp.dot(active[...], down_ref[:, columns], preferred_element_type=jnp.float32)
        keep_ref[:, columns] = part[:half]
        send_ref[:, columns] = part[half:].astype(jnp.bfloat16)


def experts(pieces, gain, w_gate, w_up, w_down, expert_count):
    local, width, hidden = w_gate.shape
    block = pieces[0].shape[0] * pieces[0].shape[1]
    count = block * len(pieces)
    extra = pieces[0].shape[2] - width
    ordered = pieces[0::2] + pieces[1::2]
    return pl.pallas_call(
        functools.partial(experts_kernel, expert_count, len(pieces)),
        out_shape=(
            jax.ShapeDtypeStruct((count // 2, width), jnp.float32),
            jax.ShapeDtypeStruct((count // 2, width), jnp.bfloat16),
        ),
        in_specs=[pl.BlockSpec(memory_space=pltpu.VMEM)] * (len(pieces) + 4),
        out_specs=[pl.BlockSpec(memory_space=pltpu.VMEM)] * 2,
        scratch_shapes=[
            pltpu.VMEM((count, width), jnp.bfloat16),
            pltpu.VMEM((count, extra), jnp.bfloat16),
            pltpu.VMEM((count, local * hidden), jnp.bfloat16),
        ],
        compiler_params=pltpu.CompilerParams(vmem_limit_bytes=40 << 20),
        cost_estimate=pl.CostEstimate(
            flops=6 * count * local * hidden * width,
            bytes_accessed=6 * local * hidden * width,
            transcendentals=count * local * hidden,
        ),
        name="experts",
    )(*ordered, gain.reshape(1, width), w_gate, w_up, w_down)


def merge(parts):
    s_top = functools.reduce(jnp.maximum, [part[0] for part in parts])
    t_top = functools.reduce(jnp.maximum, [part[2] for part in parts])
    s_scale = [jnp.exp(part[0] - s_top) for part in parts]
    s_sum = sum(scale * part[1] for scale, part in zip(s_scale, parts))
    t_sum = sum(jnp.exp(part[2] - t_top) * part[3] for part in parts)
    cross = sum(scale * part[4] for scale, part in zip(s_scale, parts))
    return jnp.stack([s_top, s_sum, t_top, t_sum, cross])


def body(
    tokens,
    routes,
    gates,
    valid,
    norm_gain,
    final_gain,
    w_gate,
    w_up,
    w_down,
    head_weight,
    student_logits,
):
    rows, width = tokens.shape
    n_dp, n_ex = lax.axis_size("dp"), lax.axis_size("expert")
    dp_at, ex_at = lax.axis_index("dp"), lax.axis_index("expert")
    local = w_gate.shape[0]
    count = rows * n_dp * n_ex
    expert_count = local * n_ex
    packed = pack(tokens, routes, gates, expert_count)

    pieces = gather_dp(jnp.stack(gather_relative(packed, "expert")))
    weights = fetch(w_gate, w_up, w_down.reshape(-1, width))
    keep, send = experts(pieces, norm_gain, *weights, expert_count)
    other = swap(send, "dp", 1).astype(jnp.float32)
    sums = (keep + other).reshape(n_dp // 2, n_ex, rows, width)
    mine = scatter_dp(sums, n_dp)
    combined = scatter_relative(mine.astype(jnp.bfloat16), "expert")
    mixed = tokens.astype(jnp.float32) + combined
    final_normed = rms_scale(mixed, final_gain).astype(jnp.bfloat16)

    along_ex = in_order(gather_relative(final_normed, "expert"), ex_at)
    everyone = in_order(gather_dp(along_ex), dp_at).reshape(count, width)
    teacher = jnp.dot(everyone, head_weight, preferred_element_type=jnp.float32)

    student = student_logits.astype(jnp.float32)
    student_top = jnp.max(student, axis=1)
    student_exp = jnp.exp(student - student_top[:, None])
    student_sum = jnp.sum(student_exp, axis=1)
    teacher_top = jnp.max(teacher, axis=1)
    teacher_sum = jnp.sum(jnp.exp(teacher - teacher_top[:, None]), axis=1)
    cross = jnp.sum(student_exp * (student - teacher), axis=1)
    own = jnp.stack([student_top, student_sum, teacher_top, teacher_sum, cross])
    own = merge(gather_relative(own, "dp"))
    s_top, s_total, t_top, t_total, cross_total = merge(gather_relative(own, "expert"))
    log_student = s_top + jnp.log(s_total)
    log_teacher = t_top + jnp.log(t_total)
    divergence = cross_total / s_total - log_student + log_teacher
    live = valid.astype(jnp.float32)
    prob = jnp.exp(student - log_student[:, None])
    shift = (cross_total / s_total)[:, None]
    grad = live[:, None] * prob * (student - teacher - shift)
    return live * divergence, grad.astype(jnp.bfloat16)


def gather_dp(block):
    size = lax.axis_size("dp")
    if size == 4:
        far = swap(block, "dp", 2)
        near = swap(block, "dp", 1)
        return [block, near, far, swap(far, "dp", 1)]
    mask = size // 2
    stacked = block[None]
    while mask >= 1:
        other = swap(stacked, "dp", mask)
        stacked = jnp.stack([stacked, other], axis=1).reshape((-1,) + block.shape)
        mask //= 2
    return [stacked[i] for i in range(size)]


def scatter_dp(blocks, size):
    mask = 2
    while mask < size:
        pairs = blocks.reshape((blocks.shape[0] // 2, 2) + blocks.shape[1:])
        other = swap(pairs[:, 1].astype(jnp.bfloat16), "dp", mask)
        blocks = pairs[:, 0] + other.astype(jnp.float32)
        mask *= 2
    return blocks[0]


def solution(mesh):
    placed = (
        P(("groups", "dp", "expert"), None),
        P("groups", None),
        P(("groups", "dp", "expert"), None),
        P("groups"),
        P(),
        P(),
        P("expert", None, "dp"),
        P("expert", None, "dp"),
        P("expert", "dp", None),
        P(None, ("dp", "expert")),
        P("groups", ("dp", "expert")),
    )
    return jax.shard_map(
        body,
        mesh=mesh,
        in_specs=placed,
        out_specs=(P("groups"), P("groups", ("dp", "expert"))),
        check_vma=False,
    )
```

```python
import functools

import jax
import jax.numpy as jnp
from jax import lax
from jax.experimental import pallas as pl
from jax.experimental.pallas import tpu as pltpu
from jax.sharding import PartitionSpec as P

epsilon = 1e-06
CHUNKS = 4
ROWS = 4
VMEM = pl.BlockSpec(memory_space=pltpu.VMEM)
HBM = pl.BlockSpec(memory_space=pltpu.HBM)


def in_hbm(*arrays):
    return [pltpu.with_memory_space_constraint(array, pltpu.HBM) for array in arrays]


def swap(value, axis, mask):
    size = lax.axis_size(axis)
    return lax.ppermute(value, axis, [(i, i ^ mask) for i in range(size)])


INPUT_GROUPS = ((0, 1, 2, 3,),)
FINAL_GROUPS = ((0,), (3,), (2, 1))


def gather(block, groups):
    n_dp, n_ex = lax.axis_size("dp"), lax.axis_size("expert")
    if (n_dp, n_ex) != (4, 4):
        return gather_any(block)
    near = {mask: swap(block, "expert", mask) for mask in (3, 2, 1)}
    near[0] = block
    own = [jnp.stack([near[i] for i in group]) for group in groups]
    far = [swap(piece, "dp", 2) for piece in own]
    pieces = [(piece, [(0, i) for i in group]) for piece, group in zip(own, groups)]
    pieces += [(piece, [(2, i) for i in group]) for piece, group in zip(far, groups)]
    names = sum(groups, ())
    pieces.append((swap(jnp.concatenate(own), "dp", 1), [(1, i) for i in names]))
    if len(groups) > 1:
        names = sum(groups[:-1], ())
        pieces.append((swap(jnp.concatenate(far[:-1]), "dp", 1), [(3, i) for i in names]))
    pieces.append((swap(far[-1], "dp", 1), [(3, i) for i in groups[-1]]))
    return pieces


def gather_any(block):
    n_dp, n_ex = lax.axis_size("dp"), lax.axis_size("expert")
    stacked = block[None]
    names = [(0, 0)]
    for axis, size in (("expert", n_ex), ("dp", n_dp)):
        mask = 1
        while mask < size:
            other = swap(stacked, axis, mask)
            stacked = jnp.concatenate([stacked, other])
            names += [(a ^ (mask if axis == "dp" else 0), b ^ (mask if axis == "expert" else 0)) for a, b in names]
            mask *= 2
    return [(stacked, names)]


def scatter(sent, kept):
    n_dp, n_ex = lax.axis_size("dp"), lax.axis_size("expert")
    if (n_dp, n_ex) != (4, 4):
        return scatter_any(sent[0], kept[0])
    rows = sent[0].shape[0] // 4
    other1 = swap(sent[0], "dp", 1)
    other0 = swap(sent[1], "dp", 1)
    away = (kept[0] + other1.astype(jnp.float32)).astype(jnp.bfloat16)
    far_a = swap(away[:rows], "dp", 2)
    far_b = swap(away[rows:], "dp", 2)
    here = kept[1] + other0.astype(jnp.float32)
    z3 = swap((here[:rows] + far_a.astype(jnp.float32)).astype(jnp.bfloat16), "expert", 3)
    rest = here[rows:] + far_b.astype(jnp.float32)
    z2 = swap(rest[:rows].astype(jnp.bfloat16), "expert", 2)
    z1 = swap(rest[rows : 2 * rows].astype(jnp.bfloat16), "expert", 1)
    return rest[2 * rows :] + z3.astype(jnp.float32) + z2.astype(jnp.float32) + z1.astype(jnp.float32)


def scatter_any(sent, kept):
    n_dp, n_ex = lax.axis_size("dp"), lax.axis_size("expert")
    total = kept + swap(sent, "dp", 1).astype(jnp.float32)
    for axis, size, least in (("dp", n_dp, 2), ("expert", n_ex, 1)):
        mask = size // 2
        while mask >= least:
            half = total.shape[0] // 2
            other = swap(total[:half].astype(jnp.bfloat16), axis, mask)
            total = total[half:] + other.astype(jnp.float32)
            mask //= 2
    return total


def row_block(name, n_dp, n_ex):
    at_dp, at_ex = name
    return ((1 - at_dp % 2) * (n_dp // 2) + n_dp // 2 - 1 - at_dp // 2) * n_ex + n_ex - 1 - at_ex


def pack_kernel(expert_count, tokens_hbm, routes_hbm, gates_hbm, packed_ref, routes_ref, gates_ref, sems):
    width = tokens_hbm.shape[1]
    copies = [
        pltpu.make_async_copy(routes_hbm, routes_ref, sems.at[0]),
        pltpu.make_async_copy(gates_hbm, gates_ref, sems.at[1]),
        pltpu.make_async_copy(tokens_hbm, packed_ref.at[:, pl.ds(0, width)], sems.at[2]),
    ]
    for copy in copies:
        copy.start()
    copies[0].wait()
    copies[1].wait()
    rows = tokens_hbm.shape[0]
    top, count = routes_ref.shape
    extra = packed_ref.shape[1] - width
    position = lax.axis_index("dp") * lax.axis_size("expert") + lax.axis_index("expert")
    column = lax.broadcasted_iota(jnp.int32, (rows, count), 1)
    row = lax.broadcasted_iota(jnp.int32, (rows, count), 0)
    pick = (column == position * rows + row).astype(jnp.float32)
    own_routes = lax.dot_general(
        pick,
        routes_ref[...].astype(jnp.float32),
        (((1,), (1,)), ((), ())),
        preferred_element_type=jnp.float32,
    )
    gates = gates_ref[...]
    weights = gates / jnp.sum(gates, axis=1, keepdims=True)
    lane = lax.broadcasted_iota(jnp.int32, (rows, extra), 1)
    expert = lax.rem(lane, expert_count).astype(jnp.float32)
    dense = jnp.zeros((rows, extra), jnp.float32)
    for k in range(top):
        dense = dense + jnp.where(own_routes[:, k : k + 1] == expert, weights[:, k : k + 1], 0.0)
    high = dense.astype(jnp.bfloat16).astype(jnp.float32)
    middle = (dense - high).astype(jnp.bfloat16).astype(jnp.float32)
    low = dense - high - middle
    side = jnp.where(lane < expert_count, high, jnp.where(lane < 2 * expert_count, middle, low))
    packed_ref[:, width:] = jnp.where(lane < 3 * expert_count, side, 0.0).astype(jnp.bfloat16)
    copies[2].wait()


def pack(tokens, routes, gates, expert_count):
    rows, width = tokens.shape
    extra = -(-3 * expert_count // 128) * 128
    return pl.pallas_call(
        functools.partial(pack_kernel, expert_count),
        out_shape=jax.ShapeDtypeStruct((rows, width + extra), jnp.bfloat16),
        in_specs=[HBM] * 3,
        out_specs=VMEM,
        scratch_shapes=[
            pltpu.VMEM(routes.shape[::-1], jnp.int32),
            pltpu.VMEM(gates.shape, jnp.float32),
            pltpu.SemaphoreType.DMA((3,)),
        ],
        compiler_params=pltpu.CompilerParams(vmem_limit_bytes=4 << 20),
        name="pack",
    )(*in_hbm(tokens, routes.T, gates))


def fetch_kernel(amount, *refs):
    sources, targets, sems = refs[:amount], refs[amount : 2 * amount], refs[2 * amount]
    copies = []
    for source, target in zip(sources, targets):
        chunk = source.shape[0] // CHUNKS
        for i in range(CHUNKS):
            rows = pl.ds(i * chunk, chunk)
            copies.append(pltpu.make_async_copy(source.at[rows], target.at[rows], sems.at[len(copies)]))
            copies[-1].start()
    for copy in copies:
        copy.wait()


def fetch(*arrays):
    size = sum(2 * array.size for array in arrays)
    return pl.pallas_call(
        functools.partial(fetch_kernel, len(arrays)),
        out_shape=tuple(pltpu.VMEM(array.shape, array.dtype) for array in arrays),
        in_specs=[HBM] * len(arrays),
        out_specs=(VMEM,) * len(arrays),
        scratch_shapes=[pltpu.SemaphoreType.DMA((CHUNKS * len(arrays),))],
        compiler_params=pltpu.CompilerParams(vmem_limit_bytes=size + (2 << 20)),
        cost_estimate=pl.CostEstimate(flops=0, bytes_accessed=size, transcendentals=0),
    )(*in_hbm(*arrays))


def experts_kernel(expert_count, places, groups, *refs):
    piece_refs, refs = refs[: len(places)], refs[len(places) :]
    gain_ref, gate_ref, up_ref, down_ref = refs[:4]
    out_refs, refs = refs[4 : 4 + groups], refs[4 + groups :]
    normed, side, active = refs
    local, width, hidden = gate_ref.shape
    steps = 4
    step = width // steps
    gain = gain_ref[...]
    for ref, blocks in zip(piece_refs, places):
        amount, rows = ref.shape[0], ref.shape[1]
        value = ref[...].astype(jnp.float32).reshape(amount * rows, ref.shape[2])
        x = value[:, :width]
        mean_square = jnp.sum(x * x, axis=1, keepdims=True) * (1.0 / width)
        scaled = x * lax.rsqrt(mean_square + epsilon) * gain
        for i, at in enumerate(blocks):
            normed[at * rows : (at + 1) * rows, :] = scaled[i * rows : (i + 1) * rows].astype(jnp.bfloat16)
            side[at * rows : (at + 1) * rows, :] = value[i * rows : (i + 1) * rows, width:].astype(jnp.bfloat16)
    first = lax.axis_index("expert") * local
    slot = lax.broadcasted_iota(jnp.int32, (side.shape[1], hidden), 0)
    for i in range(local):
        expert = first + i
        named = (slot == expert) | (slot == expert + expert_count) | (slot == expert + 2 * expert_count)
        select = jnp.where(named, 1.0, 0.0).astype(jnp.bfloat16)
        scale = jnp.dot(side[...], select, preferred_element_type=jnp.float32)
        gate_part = jnp.dot(normed[...], gate_ref[i], preferred_element_type=jnp.float32)
        up_part = jnp.dot(normed[...], up_ref[i], preferred_element_type=jnp.float32)
        value = gate_part / (1.0 + jnp.exp(-gate_part)) * up_part * scale
        active[:, i * hidden : (i + 1) * hidden] = value.astype(jnp.bfloat16)
    for i in range(steps):
        columns = slice(i * step, (i + 1) * step)
        part = jnp.dot(active[...], down_ref[:, columns], preferred_element_type=jnp.float32)
        at = 0
        for ref in out_refs:
            ref[:, columns] = part[at : at + ref.shape[0]].astype(ref.dtype)
            at += ref.shape[0]


def experts(pieces, gain, w_gate, w_up, w_down, expert_count):
    n_dp, n_ex = lax.axis_size("dp"), lax.axis_size("expert")
    local, width, hidden = w_gate.shape
    rows, full = pieces[0][0].shape[1:]
    count = rows * n_dp * n_ex
    groups = 4 if (n_dp, n_ex) == (4, 4) else 2
    kinds = [jnp.bfloat16] * (groups // 2) + [jnp.float32] * (groups // 2)
    places = tuple(tuple(row_block(name, n_dp, n_ex) for name in names) for _, names in pieces)
    outs = pl.pallas_call(
        functools.partial(experts_kernel, expert_count, places, groups),
        out_shape=[jax.ShapeDtypeStruct((count // groups, width), kind) for kind in kinds],
        in_specs=[VMEM] * (len(pieces) + 4),
        out_specs=[VMEM] * groups,
        scratch_shapes=[
            pltpu.VMEM((count, width), jnp.bfloat16),
            pltpu.VMEM((count, full - width), jnp.bfloat16),
            pltpu.VMEM((count, local * hidden), jnp.bfloat16),
        ],
        compiler_params=pltpu.CompilerParams(vmem_limit_bytes=40 << 20),
        cost_estimate=pl.CostEstimate(
            flops=6 * count * local * hidden * width,
            bytes_accessed=6 * local * hidden * width,
            transcendentals=count * local * hidden,
        ),
        name="experts",
    )(
        *[piece for piece, _ in pieces],
        gain.reshape(1, width),
        w_gate,
        w_up,
        w_down,
    )
    return outs[: groups // 2], outs[groups // 2 :]


def head_kernel(places, *refs):
    piece_refs, refs = refs[: len(places)], refs[len(places) :]
    head_ref, student_ref, teacher_ref, stats_ref, gathered = refs
    n_ex = lax.axis_size("expert")
    at_dp, at_ex = lax.axis_index("dp"), lax.axis_index("expert")
    at, owners = 0, []
    for ref, names in zip(piece_refs, places):
        amount, rows = ref.shape[0], ref.shape[1]
        value = ref[...].astype(jnp.float32).reshape(amount * rows, ref.shape[2])
        gathered[at : at + amount * rows, :] = value.astype(jnp.bfloat16)
        at += amount * rows
        owners += [(at_dp ^ by_dp) * n_ex + (at_ex ^ by_ex) for by_dp, by_ex in names]
    product = jnp.dot(gathered[...], head_ref[...], preferred_element_type=jnp.float32)
    for i, owner in enumerate(owners):
        teacher_ref[pl.ds(pl.multiple_of(owner * rows, rows), rows), :] = product[i * rows : (i + 1) * rows]
    teacher = teacher_ref[...]
    student = student_ref[...].astype(jnp.float32)
    student_top = jnp.max(student, axis=1, keepdims=True)
    student_exp = jnp.exp(student - student_top)
    student_sum = jnp.sum(student_exp, axis=1, keepdims=True)
    teacher_top = jnp.max(teacher, axis=1, keepdims=True)
    teacher_sum = jnp.sum(jnp.exp(teacher - teacher_top), axis=1, keepdims=True)
    cross = jnp.sum(student_exp * (student - teacher), axis=1, keepdims=True)
    lane = lax.broadcasted_iota(jnp.int32, (teacher.shape[0], 128), 1)
    table = jnp.zeros(lane.shape, jnp.float32)
    columns = (student_top + jnp.log(student_sum), teacher_top + jnp.log(teacher_sum), cross / student_sum)
    for i, column in enumerate(columns):
        table = jnp.where(lane == i, column, table)
    for i in range(table.shape[0] // 128):
        stats_ref[:, i * 128 : (i + 1) * 128] = table[i * 128 : (i + 1) * 128].T[: stats_ref.shape[0]]


def head(pieces, head_weight, student_logits):
    count, entries = student_logits.shape
    width = head_weight.shape[0]
    return pl.pallas_call(
        functools.partial(head_kernel, tuple(tuple(names) for _, names in pieces)),
        out_shape=(
            jax.ShapeDtypeStruct((count, entries), jnp.float32),
            jax.ShapeDtypeStruct((ROWS, count), jnp.float32),
        ),
        in_specs=[VMEM] * (len(pieces) + 2),
        out_specs=[VMEM] * 2,
        scratch_shapes=[pltpu.VMEM((count, width), jnp.bfloat16)],
        compiler_params=pltpu.CompilerParams(vmem_limit_bytes=32 << 20),
        name="head",
    )(*[piece for piece, _ in pieces], head_weight, student_logits)


def merge(parts):
    s_top = functools.reduce(jnp.maximum, [part[0:1] for part in parts])
    t_top = functools.reduce(jnp.maximum, [part[1:2] for part in parts])
    s_scale = [jnp.exp(part[0:1] - s_top) for part in parts]
    s_sum = sum(s_scale)
    t_sum = sum(jnp.exp(part[1:2] - t_top) for part in parts)
    cross = sum(scale * part[2:3] for scale, part in zip(s_scale, parts))
    return s_top + jnp.log(s_sum), t_top + jnp.log(t_sum), cross / s_sum


def final_kernel(amount, *refs):
    parts = [refs[0][i] for i in range(refs[0].shape[0])]
    valid_ref, student_ref, teacher_ref, kl_ref, grad_ref = refs[amount:]
    log_student, log_teacher, shift = merge(parts)
    live = valid_ref[...].astype(jnp.float32)
    kl_ref[...] = live * (shift - log_student + log_teacher)
    count = live.shape[1]
    for i in range(count // 128):
        lanes = slice(i * 128, (i + 1) * 128)
        row = lax.broadcasted_iota(jnp.int32, (128, 128), 0)
        table = jnp.where(row == 0, log_student[:, lanes], jnp.where(row == 1, shift[:, lanes], live[:, lanes])).T
        student = student_ref[lanes, :].astype(jnp.float32)
        grad = table[:, 2:3] * jnp.exp(student - table[:, 0:1]) * (student - teacher_ref[lanes, :] - table[:, 1:2])
        grad_ref[lanes, :] = grad.astype(jnp.bfloat16)


def final(parts, valid, student_logits, teacher):
    count = valid.shape[0]
    kl, grad = pl.pallas_call(
        functools.partial(final_kernel, len(parts)),
        out_shape=(
            jax.ShapeDtypeStruct((1, count), jnp.float32),
            jax.ShapeDtypeStruct(student_logits.shape, jnp.bfloat16),
        ),
        in_specs=[VMEM] * (len(parts) + 3),
        out_specs=[VMEM] * 2,
        compiler_params=pltpu.CompilerParams(vmem_limit_bytes=24 << 20),
        name="final",
    )(*parts, valid.reshape(1, count), student_logits, teacher)
    return kl.reshape(count), grad


def body(
    tokens,
    routes,
    gates,
    valid,
    norm_gain,
    final_gain,
    w_gate,
    w_up,
    w_down,
    head_weight,
    student_logits,
):
    expert_count = w_gate.shape[0] * lax.axis_size("expert")
    packed = pack(tokens, routes, gates, expert_count)
    pieces = gather(packed, INPUT_GROUPS)
    (w_gate,) = fetch(w_gate)
    w_up, w_down = fetch(w_up, w_down.reshape(-1, tokens.shape[1]))
    sent, kept = experts(pieces, norm_gain, w_gate, w_up, w_down, expert_count)
    combined = scatter(sent, kept)
    mixed = tokens.astype(jnp.float32) + combined
    mean_square = jnp.mean(mixed * mixed, axis=-1, keepdims=True)
    final_normed = (mixed * lax.rsqrt(mean_square + epsilon) * final_gain).astype(jnp.bfloat16)
    pieces = gather(final_normed, FINAL_GROUPS)
    teacher, stats = head(pieces, head_weight, student_logits)
    ranks = lax.axis_size("dp") * lax.axis_size("expert")
    copies = jnp.broadcast_to(stats[None], (ranks,) + stats.shape)
    shared = lax.all_to_all(copies, ("dp", "expert"), 0, 0, tiled=True)
    parts = [shared]
    return final(parts, valid, student_logits, teacher)


def solution(mesh):
    placed = (
        P(("groups", "dp", "expert"), None),
        P("groups", None),
        P(("groups", "dp", "expert"), None),
        P("groups"),
        P(),
        P(),
        P("expert", None, "dp"),
        P("expert", None, "dp"),
        P("expert", "dp", None),
        P(None, ("dp", "expert")),
        P("groups", ("dp", "expert")),
    )
    return jax.shard_map(
        body,
        mesh=mesh,
        in_specs=placed,
        out_specs=(P("groups"), P("groups", ("dp", "expert"))),
        check_vma=False,
    )
```
